256 devices in a mesh: row: 16 (over z_lo, x, core), col: 4 (over y), item: 4 (over z_hi).
Axes of the slice: x: 4, y: 4, z: 8 (z_hi: 4, z_lo: 2; z = z_hi * 2 + z_lo), core: 2. Of those that a mesh axis runs over, the one named last changes fastest.
Arguments:
- tokens: bfloat16 [4, 16, 64, 2432], P('item', 'row', 'col'), may hold values from -6 to 6
- text_keys_values: bfloat16 [4, 154, 2, 2048], P('item', None, None, 'row'), may hold values from -200 to 200
- text_length: int32 [4], P('item'), may hold values from 2 to 154, as said below
- modulation: float32 [4, 8, 2432], P('item'), may hold values from -4 to 4
- input_weight: bfloat16 [2432, 3, 2048], P(None, None, 'row'), may hold values from -0.125 to 0.125
- norm_gain: float32 [2, 64], replicated, may hold values from 1 to 3
- output_weight: bfloat16 [2048, 2432], P('row'), may hold values from -0.125 to 0.125
- up_weight: bfloat16 [2432, 9728], P(None, 'row'), may hold values from -0.125 to 0.125
- down_weight: bfloat16 [9728, 2432], P('row'), may hold values from -0.0625 to 0.0625
- final_weight: bfloat16 [2432, 64], replicated, may hold values from -0.125 to 0.125
- step_index: int32 [1], replicated, may hold values from 0 to 27
- latent: float32 [4, 16, 4096], P('item', 'row', 'col'), may hold values from -6 to 6
Outputs:
- tokens_out: bfloat16 [4, 16, 64, 2432], P('item', 'row', 'col')
- velocity: float32 [4, 16, 4096], P('item', 'row', 'col')
- latent_next: float32 [4, 16, 4096], P('item', 'row', 'col')
The draws below stay inside these ranges and needn't reach their ends.
Inputs may be any that keep to these rules, and one draw needn't show every extreme that they name: `text_length`: at least one sequence has all 154 text tokens valid.
All inputs are finite; a program needn't handle non-finite values.
Results may differ from the reference program's by a relative error of at most 0.024.
Values may be sent and summed in bfloat16 or wider, within the bound.
A program may use at most 64 MiB of HBM per device.

```python
import math
import jax
import jax.numpy as jnp
from jax import lax

D = 2432
HEADS = 32
HD = 64
FF = 9728
PC = 64
TXT = 154
STEPS = 28
GH = 16
GW = 64
IMG = 1024
SEQS = 4
N_ROW = 16


def draw_text_length(key, part):
    lengths = jax.random.randint(key, (SEQS,), 2, TXT + 1)
    chosen = jax.random.randint(jax.random.fold_in(key, 7), (), 0, SEQS)
    return jnp.where(jnp.arange(SEQS) == chosen, TXT, lengths).astype(jnp.int32)


def draw_text_keys_values(key, part):
    sampled = jnp.clip(jax.random.normal(key, (SEQS, TXT, 2, HEADS * HD), jnp.float32), -6.0, 6.0) * 2.5
    return sampled.astype(jnp.bfloat16)


def steps_of(own_key, dims, shards, least, high):
    gain = 1.0
    for axis_at, shards_of in shards:
        steps = jax.random.uniform(jax.random.fold_in(jax.random.fold_in(own_key, 6), axis_at), (shards_of,), jnp.float32, least / len(shards), high / len(shards))
        gain = gain * jnp.repeat(jnp.exp(steps), dims[axis_at] // shards_of).reshape((-1,) + (1,) * (len(dims) - 1 - axis_at))
    return gain


def noise(rng, extent, deviation, limit, pieces=(), kind=jnp.bfloat16):
    factor_of = steps_of(rng, extent, pieces, -0.22, 0.18) if pieces else 1.0
    drawn = jax.random.normal(rng, extent, jnp.float32) * deviation * factor_of
    return jnp.minimum(jnp.maximum(drawn, -limit), limit).astype(kind)


def setup_inputs(seed: int = 0) -> dict:
    key_list = jax.random.split(jax.random.key(seed), 13)
    return {
        "tokens": noise(key_list[0], (SEQS, GH, GW, D), 1.0, 6.0, ((0, 4), (1, 16), (2, 4))),
        "text_keys_values": draw_text_keys_values(jax.random.fold_in(key_list[12], 71), 0),
        "text_length": draw_text_length(jax.random.fold_in(key_list[12], 71), 0),
        "modulation": noise(key_list[3], (SEQS, 8, D), 0.7, 4.0, ((0, 4),), jnp.float32),
        "input_weight": noise(key_list[4], (D, 3, HEADS * HD), D ** -0.5, 0.125, ((2, 16),)),
        "norm_gain": jnp.clip(jnp.exp(jax.random.uniform(key_list[5], (2, HD), jnp.float32, math.log(1.0), math.log(3.0))), 1.0, 3.0),
        "output_weight": noise(key_list[6], (HEADS * HD, D), (HEADS * HD) ** -0.5, 0.125, ((0, 16),)),
        "up_weight": noise(key_list[7], (D, FF), D ** -0.5, 0.125, ((1, 16),)),
        "down_weight": noise(key_list[8], (FF, D), FF ** -0.5, 0.0625, ((0, 16),)),
        "final_weight": noise(key_list[9], (D, PC), D ** -0.5, 0.125),
        "step_index": jax.random.randint(key_list[10], (1,), 0, STEPS).astype(jnp.int32),
        "latent": noise(key_list[11], (SEQS, GH, GW * PC), 1.0, 6.0, ((0, 4), (1, 16), (2, 4)), jnp.float32),
    }


EPSILON = 1e-06
SHIFT_FACTOR = 3.0
GUIDANCE = 4.5
MASKED = -1e+30

def layer_norm(values):
    center = values - lax.optimization_barrier(jnp.mean(values, axis=-1, keepdims=True))
    spread = lax.optimization_barrier(jnp.mean(center * center, axis=-1, keepdims=True))
    return center * lax.rsqrt(spread + EPSILON)

def modulate(values, shift_term, scale_term):
    return (layer_norm(values) * (1.0 + scale_term) + shift_term).astype(jnp.bfloat16)

def root_norm(values, gain_row):
    return values * lax.rsqrt(lax.optimization_barrier(jnp.mean(values * values, axis=-1, keepdims=True)) + EPSILON) * gain_row

def noise_level(position):
    linear = 1.0 - position / STEPS
    return SHIFT_FACTOR * linear / (1.0 + (SHIFT_FACTOR - 1.0) * linear)

def one_sequence(tile_grid, text_pairs, length, mod_rows, input_weight, norm_gain, output_weight, up_weight, down_weight, final_weight):
    states = tile_grid.reshape(IMG, D).astype(jnp.float32)
    attn_input = modulate(states, mod_rows[0], mod_rows[1])
    projected = jnp.dot(attn_input, input_weight.reshape(D, 3 * HEADS * HD), preferred_element_type=jnp.float32)
    projected = projected.reshape(IMG, 3, HEADS, HD)
    queries = root_norm(projected[:, 0], norm_gain[0]).astype(jnp.bfloat16)
    keys_image = root_norm(projected[:, 1], norm_gain[1]).astype(jnp.bfloat16)
    values_image = projected[:, 2].astype(jnp.bfloat16)
    keys_text = text_pairs[:, 0].reshape(TXT, HEADS, HD)
    values_text = text_pairs[:, 1].reshape(TXT, HEADS, HD)
    keep_mask = jnp.concatenate([jnp.ones((IMG,), dtype=bool), jnp.arange(TXT) < length])
    all_keys = jnp.concatenate([keys_image, keys_text], axis=0)
    all_values = jnp.concatenate([values_image, values_text], axis=0)

    def attend(head_index):
        query_head = queries[:, head_index]
        key_head = all_keys[:, head_index]
        value_head = all_values[:, head_index]
        scores = jnp.dot(query_head, key_head.T, preferred_element_type=jnp.float32) * HD ** (-0.5)
        scores = jnp.where(keep_mask[None, :], scores, MASKED)
        largest = lax.optimization_barrier(jnp.max(scores, axis=1, keepdims=True))
        weights = jnp.exp(scores - largest)
        total_mass = lax.optimization_barrier(jnp.sum(weights, axis=1, keepdims=True))
        mixture = jnp.dot(weights.astype(jnp.bfloat16), value_head, preferred_element_type=jnp.float32)
        return (mixture / total_mass).astype(jnp.bfloat16)
    heads_out = lax.map(attend, jnp.arange(HEADS))
    attended = heads_out.transpose(1, 0, 2).reshape(IMG, HEADS * HD)
    group_width = HEADS * HD // N_ROW
    attention = jnp.zeros((IMG, D), jnp.float32)
    for group_index in range(N_ROW):
        low = group_index * group_width
        partial_value = jnp.dot(attended[:, low:low + group_width], output_weight[low:low + group_width], preferred_element_type=jnp.float32)
        attention = attention + lax.optimization_barrier(partial_value.astype(jnp.bfloat16)).astype(jnp.float32)
    middle = states + mod_rows[2] * attention
    feed_input = modulate(middle, mod_rows[3], mod_rows[4])
    hidden = jax.nn.gelu(jnp.dot(feed_input, up_weight, preferred_element_type=jnp.float32), approximate=True).astype(jnp.bfloat16)
    hidden_width = FF // N_ROW
    feed = jnp.zeros((IMG, D), jnp.float32)
    for group_index in range(N_ROW):
        low = group_index * hidden_width
        partial_value = jnp.dot(hidden[:, low:low + hidden_width], down_weight[low:low + hidden_width], preferred_element_type=jnp.float32)
        feed = feed + lax.optimization_barrier(partial_value.astype(jnp.bfloat16)).astype(jnp.float32)
    leaving = middle + mod_rows[5] * feed
    final_input = modulate(leaving, mod_rows[6], mod_rows[7])
    raw_velocity = jnp.dot(final_input, final_weight, preferred_element_type=jnp.float32).reshape(GH, GW * PC)
    return (leaving.astype(jnp.bfloat16).reshape(GH, GW, D), raw_velocity)

def reference(tokens, text_keys_values, text_length, modulation, input_weight, norm_gain, output_weight, up_weight, down_weight, final_weight, step_index, latent):
    outputs = []
    velocities = []
    for sequence in range(SEQS):
        leaving, raw_velocity = one_sequence(tokens[sequence], text_keys_values[sequence], text_length[sequence], modulation[sequence], input_weight, norm_gain, output_weight, up_weight, down_weight, final_weight)
        outputs.append(leaving)
        velocities.append(raw_velocity)
    stacked = jnp.stack(velocities).reshape(SEQS // 2, 2, GH, GW * PC)
    guided = stacked[:, 0]
    unguided = stacked[:, 1]
    combined = unguided + GUIDANCE * (guided - unguided)
    velocity = jnp.stack([combined, combined], axis=1).reshape(SEQS, GH, GW * PC)
    position = step_index[0].astype(jnp.float32)
    step_size = noise_level(position + 1.0) - noise_level(position)
    return (jnp.stack(outputs), velocity, latent + step_size * velocity)
```

```python
import functools

import jax
import jax.numpy as jnp
from jax import lax
from jax.experimental import pallas as pl
from jax.experimental.pallas import tpu as pltpu
from jax.sharding import PartitionSpec as P

HD = 64
STEPS = 28
EPSILON = 1e-06
SHIFT_FACTOR = 3.0
GUIDANCE = 4.5
MASKED = -1e30
MESH = pl.DeviceIdType.MESH
BF16 = jnp.bfloat16
F32 = jnp.float32

PEERS = ((1, 2), (0, 2), (1, 1), (1, 3), (0, 1), (0, 3), (1, 0))
TEXT_PAD = 160


def slot_of(dz, dx):
    return (dz % 2) * 4 + dx % 4


def layer_norm(values):
    center = values - jnp.mean(values, axis=-1, keepdims=True)
    spread = jnp.mean(center * center, axis=-1, keepdims=True)
    return center * lax.rsqrt(spread + EPSILON)


def modulate(values, shift_term, scale_term):
    return (layer_norm(values) * (1.0 + scale_term) + shift_term).astype(BF16)


def noise_level(position):
    linear = 1.0 - position / STEPS
    return SHIFT_FACTOR * linear / (1.0 + (SHIFT_FACTOR - 1.0) * linear)


def nt_dot(left, right):
    return lax.dot_general(left, right, (((1,), (1,)), ((), ())), preferred_element_type=F32)


def layer_kernel(
    length_ref, step_ref, tok_hbm, text_hbm, mod_hbm, win_hbm, gain_hbm, wo_hbm, wu_hbm, wd_hbm, wf_hbm, lat_hbm,
    out_tok, out_vel, out_lat,
    tok, text, mod, wi, gain, wo, wu, wd, wf, lat,
    g1, g2, p1, p2, r1, r2, kvr, kvs, qb, qs, ab, ats, s_max, s_sum, s_acc, vraw, vx, vr,
    local_sem, w_send, w_recv, g1_send, g1_recv, kv_send, kv_recv, q_send, q_recv, a_send, a_recv,
    r1_send, r1_recv, g2_send, g2_recv, r2_send, r2_recv, v_send, v_recv,
):
    tile, width = tok.shape
    half = tile * 8
    ff = wu_hbm.shape[0]
    row = lax.axis_index("row")
    col = lax.axis_index("col")
    item = lax.axis_index("item")
    z, x, k = row // 8, (row // 2) % 4, row % 2

    def device(dz=0, dx=0, dk=0, dc=0, other_item=False):
        row_to = ((z + dz) % 2) * 8 + ((x + dx) % 4) * 2 + (k + dk) % 2
        item_to = item + 1 - 2 * (item % 2) if other_item else item
        return (row_to, (col + dc) % 4, item_to)

    def send(src, dst, send_sem, recv_sem, to):
        copy = pltpu.make_async_remote_copy(
            src_ref=src, dst_ref=dst, send_sem=send_sem, recv_sem=recv_sem, device_id=to, device_id_type=MESH
        )
        copy.start()
        return copy

    pairs = [(tok_hbm, tok), (mod_hbm, mod)]
    pairs += [(win_hbm.at[j], wi.at[:, pl.ds(128 * j, 128)]) for j in range(3)]
    pairs += [(text_hbm, text), (gain_hbm, gain), (wo_hbm, wo.at[pl.ds(0, 128)])]
    pairs += [(wu_hbm, wu.at[pl.ds(0, ff)]), (wd_hbm, wd.at[pl.ds(0, ff)]), (wf_hbm, wf), (lat_hbm, lat)]
    loads = [pltpu.make_async_copy(src, dst, local_sem.at[j]) for j, (src, dst) in enumerate(pairs)]
    for load in loads:
        load.start()

    friends = [device(dz, dx) for dz, dx in PEERS] + [device(dk=1), device(other_item=True)]
    friends += [device(dk=dk, dc=dc) for dc in (1, 2, 3) for dk in (0, 1)]
    barrier = pltpu.get_barrier_semaphore()
    for friend in friends:
        pl.semaphore_signal(barrier, inc=1, device_id=friend, device_id_type=MESH)

    loads[0].wait()
    loads[1].wait()
    states = tok[...].astype(F32)
    g1[pl.ds(0, tile), :] = modulate(states, mod[0:1, :], mod[1:2, :])
    pl.semaphore_wait(barrier, len(friends))

    def spread(buf, send_sems, recv_sems):
        copies = []
        for n, (dz, dx) in enumerate(PEERS):
            to = slot_of(dz, -dx)
            copies.append(
                send(
                    buf.at[pl.ds(0, tile)], buf.at[pl.ds(to * tile, tile)], send_sems.at[n], recv_sems.at[n],
                    device(dz, dx),
                )
            )
        return copies

    gather1 = spread(g1, g1_send, g1_recv)
    sibling = device(dk=1)
    weight_pairs = [(win_hbm.at[j], wi.at[:, pl.ds(384 + 128 * j, 128)]) for j in range(3)]
    weight_pairs += [(wo_hbm, wo.at[pl.ds(128, 128)]), (wu_hbm, wu.at[pl.ds(ff, ff)]), (wd_hbm, wd.at[pl.ds(ff, ff)])]
    shared = [send(src, dst, w_send.at[j], w_recv.at[j], sibling) for j, (src, dst) in enumerate(weight_pairs)]

    loads[5].wait()
    loads[6].wait()
    text_rows = text.shape[0]
    picked = lax.broadcasted_iota(jnp.int32, (TEXT_PAD, text_rows), 1)
    wanted = 2 * lax.broadcasted_iota(jnp.int32, (TEXT_PAD, text_rows), 0)
    text_all = text[...]
    key_text = jnp.dot((picked == wanted).astype(BF16), text_all, preferred_element_type=F32).astype(BF16)
    value_text = jnp.dot((picked == wanted + 1).astype(BF16), text_all, preferred_element_type=F32).astype(BF16)
    gains = gain[...]
    gain_rows = jnp.concatenate([gains, gains], axis=1)
    lane = lax.broadcasted_iota(jnp.int32, (1, 128), 1)
    head_masks = ((lane < HD).astype(BF16), (lane >= HD).astype(BF16))

    def root_norm(values, gain_row):
        squares = values * values
        first = jnp.sum(jnp.where(lane < HD, squares, 0.0), axis=1, keepdims=True)
        second = jnp.sum(jnp.where(lane < HD, 0.0, squares), axis=1, keepdims=True)
        mean = jnp.where(lane < HD, first, second) * (1.0 / HD)
        return values * lax.rsqrt(mean + EPSILON) * gain_row

    for j in (2, 3, 4):
        loads[j].wait()
    for copy in shared[:3]:
        copy.wait()
    for copy in gather1:
        copy.wait()
    projected = jnp.dot(g1[...], wi[...], preferred_element_type=F32)

    kvs[:, 0:128] = root_norm(projected[:, 512:640], gain_rows[1:2]).astype(BF16)
    kvs[:, 128:256] = projected[:, 640:768].astype(BF16)
    kvr[0, 0, :, 0:128] = root_norm(projected[:, 128:256], gain_rows[1:2]).astype(BF16)
    kvr[0, 0, :, 128:256] = projected[:, 256:384].astype(BF16)
    kv_copies = {}
    for dc in (2, 1, 3):
        kv_copies[4 - dc] = [
            send(kvr.at[0, 0], kvr.at[4 - dc, 0], kv_send.at[dc, 0], kv_recv.at[4 - dc, 0], device(dc=dc)),
            send(kvs, kvr.at[4 - dc, 1], kv_send.at[dc, 1], kv_recv.at[4 - dc, 1], device(dk=1, dc=dc)),
        ]
    own_pair = send(kvs, kvr.at[0, 1], kv_send.at[0, 1], kv_recv.at[0, 1], sibling)
    qs[...] = (root_norm(projected[:, 384:512], gain_rows[0:1]) * HD ** (-0.5)).astype(BF16)
    q_copy = send(qs, qb.at[pl.ds(half, half)], q_send, q_recv, sibling)
    qb[pl.ds(0, half), :] = (root_norm(projected[:, 0:128], gain_rows[0:1]) * HD ** (-0.5)).astype(BF16)

    def attend(keys, values, chunks, keep=None):
        for n in chunks:
            rows = pl.ds(n * half, half)
            query = qb[pl.ds((n % 2) * half, half), :] * head_masks[n // 2]
            scores = nt_dot(query, keys)
            if keep is not None:
                scores = jnp.where(keep, scores, MASKED)
            old = s_max[rows, :]
            new = jnp.maximum(old, jnp.max(scores, axis=1, keepdims=True))
            factor = jnp.exp(old - new)
            weights = jnp.exp(scores - new[:, 0:1])
            s_max[rows, :] = new
            s_sum[rows, :] = s_sum[rows, :] * factor + jnp.sum(weights, axis=1, keepdims=True)
            s_acc[rows, :] = s_acc[rows, :] * factor + jnp.dot(
                weights.astype(BF16), values, preferred_element_type=F32
            )

    s_max[...] = jnp.full_like(s_max, MASKED)
    s_sum[...] = jnp.zeros_like(s_sum)
    s_acc[...] = jnp.zeros_like(s_acc)
    keep = lax.broadcasted_iota(jnp.int32, (1, TEXT_PAD), 1) < length_ref[0]
    attend(kvr[0, 0, :, 0:128], kvr[0, 0, :, 128:256], (0, 2))
    attend(key_text, value_text, (0, 2), keep)
    q_copy.wait()
    own_pair.wait()
    attend(kvr[0, 0, :, 0:128], kvr[0, 0, :, 128:256], (1, 3))
    attend(key_text, value_text, (1, 3), keep)
    attend(kvr[0, 1, :, 0:128], kvr[0, 1, :, 128:256], (1, 3, 0, 2))
    for dc in (1, 3, 2):
        for copy in kv_copies[dc]:
            copy.wait()
        for part in range(2):
            attend(kvr[dc, part, :, 0:128], kvr[dc, part, :, 128:256], (1, 3, 0, 2))

    def attended(parity):
        low, high = pl.ds(parity * half, half), pl.ds((2 + parity) * half, half)
        first = s_acc[low, :] / s_sum[low, :]
        second = s_acc[high, :] / s_sum[high, :]
        return jnp.where(lane < HD, first, second).astype(BF16)

    ats[...] = attended(1)
    a_copy = send(ats, ab.at[:, pl.ds(128, 128)], a_send, a_recv, sibling)
    ab[:, 0:128] = attended(0)
    loads[7].wait()
    shared[3].wait()
    a_copy.wait()

    columns = [(n, min(512, width - n)) for n in range(0, width, 512)]

    def scatter(left, weight, part, arrive, send_sems, recv_sems):
        copies = []
        for c, (start, size) in enumerate(columns):
            cols = pl.ds(start, size)
            part[:, cols] = jnp.dot(left, weight[:, cols], preferred_element_type=F32).astype(BF16)
            for n, (dz, dx) in enumerate(PEERS):
                src = part.at[pl.ds(slot_of(dz, dx) * tile, tile), cols]
                dst = arrive.at[pl.ds(slot_of(dz, -dx) * tile, tile), cols]
                copies.append(send(src, dst, send_sems.at[c, n], recv_sems.at[c, n], device(dz, dx)))
        return copies

    def collect(copies, part, arrive):
        for copy in copies:
            copy.wait()
        total = part[pl.ds(0, tile), :].astype(F32)
        for n in range(1, 8):
            total = total + arrive[pl.ds(n * tile, tile), :].astype(F32)
        return total

    scatter1 = scatter(ab[...], wo, p1, r1, r1_send, r1_recv)
    attention = collect(scatter1, p1, r1)
    middle = tok[...].astype(F32) + mod[2:3, :] * attention
    g2[pl.ds(0, tile), :] = modulate(middle, mod[3:4, :], mod[4:5, :])
    gather2 = spread(g2, g2_send, g2_recv)
    loads[8].wait()
    loads[9].wait()
    shared[4].wait()
    shared[5].wait()
    for copy in gather2:
        copy.wait()
    hidden = jax.nn.gelu(nt_dot(g2[...], wu[...]), approximate=True).astype(BF16)
    scatter2 = scatter(hidden, wd, p2, r2, r2_send, r2_recv)
    feed = collect(scatter2, p2, r2)
    leaving = middle + mod[5:6, :] * feed
    out_tok[...] = leaving.astype(BF16)
    final_input = modulate(leaving, mod[6:7, :], mod[7:8, :])
    loads[10].wait()
    loads[11].wait()
    vraw[...] = nt_dot(final_input, wf[...])
    pairs_of_tokens = tile // 2
    vx[...] = jnp.concatenate(
        [vraw[pl.ds(0, pairs_of_tokens, stride=2), :], vraw[pl.ds(1, pairs_of_tokens, stride=2), :]], axis=1
    )
    v_copy = send(vx, vr, v_send, v_recv, device(other_item=True))
    v_copy.wait()
    mine, theirs = vx[...], vr[...]
    is_guided = jnp.full(mine.shape, item % 2, jnp.int32) == 0
    guided = jnp.where(is_guided, mine, theirs)
    unguided = jnp.where(is_guided, theirs, mine)
    velocity = unguided + GUIDANCE * (guided - unguided)
    position = jnp.full(mine.shape, step_ref[0], jnp.int32).astype(F32)
    step_size = noise_level(position + 1.0) - noise_level(position)
    out_vel[...] = velocity
    out_lat[...] = lat[...] + step_size * velocity


def on_device(
    tokens,
    text_keys_values,
    text_length,
    modulation,
    input_weight,
    norm_gain,
    output_weight,
    up_weight,
    down_weight,
    final_weight,
    step_index,
    latent,
):
    tile = tokens.shape[1] * tokens.shape[2]
    width = tokens.shape[3]
    ff = up_weight.shape[1]
    half = 8 * tile
    chunks = -(-width // 512)
    operands = (
        text_length,
        step_index,
        tokens.reshape(tile, width),
        text_keys_values.reshape(-1, text_keys_values.shape[3]),
        modulation.reshape(8, width),
        input_weight.transpose(1, 0, 2),
        norm_gain,
        output_weight,
        up_weight.T,
        down_weight,
        final_weight.T,
        latent.reshape(-1, 128),
    )
    lat_shape = operands[-1].shape
    vmem = pltpu.VMEM
    dma = pltpu.SemaphoreType.DMA
    scratch = [
        vmem((tile, width), BF16),
        vmem(operands[3].shape, BF16),
        vmem((8, width), F32),
        vmem((width, 768), BF16),
        vmem(norm_gain.shape, F32),
        vmem((256, width), BF16),
        vmem((2 * ff, width), BF16),
        vmem((2 * ff, width), BF16),
        vmem((final_weight.shape[1], width), BF16),
        vmem(lat_shape, F32),
    ]
    scratch += [vmem((half, width), BF16)] * 6
    scratch += [
        vmem((4, 2, half, 256), BF16),
        vmem((half, 256), BF16),
        vmem((2 * half, 128), BF16),
        vmem((half, 128), BF16),
        vmem((half, 256), BF16),
        vmem((half, 128), BF16),
        vmem((4 * half, 128), F32),
        vmem((4 * half, 128), F32),
        vmem((4 * half, 128), F32),
        vmem((tile, final_weight.shape[1]), F32),
        vmem(lat_shape, F32),
        vmem(lat_shape, F32),
    ]
    scratch += [dma((12,)), dma((6,)), dma((6,)), dma((7,)), dma((7,)), dma((4, 2)), dma((4, 2))]
    scratch += [dma, dma, dma, dma, dma((chunks, 7)), dma((chunks, 7)), dma((7,)), dma((7,))]
    scratch += [dma((chunks, 7)), dma((chunks, 7)), dma, dma]
    smem = pl.BlockSpec(memory_space=pltpu.SMEM)
    hbm = pl.BlockSpec(memory_space=pl.ANY)
    whole = pl.BlockSpec(memory_space=pltpu.VMEM)
    tokens_out, velocity, latent_next = pl.pallas_call(
        layer_kernel,
        out_shape=(
            jax.ShapeDtypeStruct((tile, width), BF16),
            jax.ShapeDtypeStruct(lat_shape, F32),
            jax.ShapeDtypeStruct(lat_shape, F32),
        ),
        in_specs=[smem, smem] + [hbm] * 10,
        out_specs=(whole, whole, whole),
        scratch_shapes=scratch,
        compiler_params=pltpu.CompilerParams(
            collective_id=0, has_side_effects=True, vmem_limit_bytes=56 * 1024 * 1024
        ),
        name="layer",
    )(*operands)
    return (tokens_out.reshape(tokens.shape), velocity.reshape(latent.shape), latent_next.reshape(latent.shape))


def solution(mesh):
    in_specs = (
        P("item", "row", "col", None),
        P("item", None, None, "row"),
        P("item"),
        P("item", None, None),
        P(None, None, "row"),
        P(),
        P("row", None),
        P(None, "row"),
        P("row", None),
        P(),
        P(),
        P("item", "row", "col"),
    )
    out_specs = (P("item", "row", "col", None), P("item", "row", "col"), P("item", "row", "col"))
    return jax.shard_map(
        on_device, mesh=mesh, in_specs=in_specs, out_specs=out_specs, check_vma=False
    )
```

```python
import functools

import jax
import jax.numpy as jnp
from jax import lax
from jax.experimental import pallas as pl
from jax.experimental.pallas import tpu as pltpu
from jax.sharding import PartitionSpec as P

HD = 64
STEPS = 28
EPSILON = 1e-06
SHIFT_FACTOR = 3.0
GUIDANCE = 4.5
MASKED = -1e30
MESH = pl.DeviceIdType.MESH
BF16 = jnp.bfloat16
F32 = jnp.float32

PEERS = ((1, 2), (0, 2), (1, 1), (1, 3), (0, 1), (0, 3), (1, 0))
TEXT_PAD = 160


def slot_of(dz, dx):
    return (dz % 2) * 4 + dx % 4


def layer_norm(values):
    center = values - jnp.mean(values, axis=-1, keepdims=True)
    spread = jnp.mean(center * center, axis=-1, keepdims=True)
    return center * lax.rsqrt(spread + EPSILON)


def modulate(values, shift_term, scale_term):
    return (layer_norm(values) * (1.0 + scale_term) + shift_term).astype(BF16)


def noise_level(position):
    linear = 1.0 - position / STEPS
    return SHIFT_FACTOR * linear / (1.0 + (SHIFT_FACTOR - 1.0) * linear)


def nt_dot(left, right):
    return lax.dot_general(left, right, (((1,), (1,)), ((), ())), preferred_element_type=F32)


def layer_kernel(
    length_ref, tok_hbm, text_hbm, mod_hbm, win_hbm, gain_hbm, wo_hbm, wu_hbm, wd_hbm, wf_hbm,
    out_tok, out_mine, out_theirs,
    tok, text, mod, wi, gain, wo, wu, wd, wf,
    g1, g2, p1, p2, r1, r2, kvr, kvs, qb, qs, ab, ats, s_max, s_sum, s_acc, vraw, vx, vr, text_keys, text_values,
    local_sem, w_send, w_recv, g1_send, g1_recv, kv_send, kv_recv, q_send, q_recv, a_send, a_recv,
    r1_send, r1_recv, g2_send, g2_recv, r2_send, r2_recv, v_send, v_recv,
):
    tile, width = tok.shape
    half = tile * 8
    ff = wu_hbm.shape[0]
    row = lax.axis_index("row")
    col = lax.axis_index("col")
    item = lax.axis_index("item")
    z, x, k = row // 8, (row // 2) % 4, row % 2

    def device(dz=0, dx=0, dk=0, dc=0, other_item=False):
        row_to = ((z + dz) % 2) * 8 + ((x + dx) % 4) * 2 + (k + dk) % 2
        item_to = item + 1 - 2 * (item % 2) if other_item else item
        return (row_to, (col + dc) % 4, item_to)

    def send(src, dst, send_sem, recv_sem, to):
        copy = pltpu.make_async_remote_copy(
            src_ref=src, dst_ref=dst, send_sem=send_sem, recv_sem=recv_sem, device_id=to, device_id_type=MESH
        )
        copy.start()
        return copy

    pairs = [(tok_hbm, tok), (mod_hbm, mod)]
    pairs += [(win_hbm.at[j], wi.at[:, pl.ds(128 * j, 128)]) for j in range(3)]
    pairs += [(text_hbm, text), (gain_hbm, gain), (wo_hbm, wo.at[pl.ds(0, 128)])]
    pairs += [(wu_hbm, wu.at[pl.ds(0, ff)]), (wd_hbm, wd.at[pl.ds(0, ff)]), (wf_hbm, wf)]
    loads = [pltpu.make_async_copy(src, dst, local_sem.at[j]) for j, (src, dst) in enumerate(pairs)]
    for load in loads:
        load.start()

    friends = [device(dz, dx) for dz, dx in PEERS] + [device(dk=1), device(other_item=True)]
    friends += [device(dk=dk, dc=dc) for dc in (1, 2, 3) for dk in (0, 1)]
    barrier = pltpu.get_barrier_semaphore()
    for friend in friends:
        pl.semaphore_signal(barrier, inc=1, device_id=friend, device_id_type=MESH)

    loads[0].wait()
    loads[1].wait()
    states = tok[...].astype(F32)
    g1[pl.ds(0, tile), :] = modulate(states, mod[0:1, :], mod[1:2, :])
    pl.semaphore_wait(barrier, len(friends))

    parts = [pl.ds(n, min(640, width - n)) for n in range(0, width, 640)]

    def spread(buf, send_sems, recv_sems):
        copies = []
        for c, cols in enumerate(parts):
            for n, (dz, dx) in enumerate(PEERS):
                src = buf.at[pl.ds(0, tile), cols]
                dst = buf.at[pl.ds(slot_of(dz, -dx) * tile, tile), cols]
                copies.append(send(src, dst, send_sems.at[c, n], recv_sems.at[c, n], device(dz, dx)))
        return copies

    def project(buf, copies, product):
        total = None
        for c, cols in enumerate(parts):
            for copy in copies[7 * c : 7 * c + 7]:
                copy.wait()
            term = product(buf[:, cols], cols)
            total = term if total is None else total + term
        return total

    gather1 = spread(g1, g1_send, g1_recv)
    sibling = device(dk=1)
    weight_pairs = [(win_hbm.at[j], wi.at[:, pl.ds(384 + 128 * j, 128)]) for j in range(3)]
    weight_pairs += [(wo_hbm, wo.at[pl.ds(128, 128)]), (wu_hbm, wu.at[pl.ds(ff, ff)]), (wd_hbm, wd.at[pl.ds(ff, ff)])]
    shared = [send(src, dst, w_send.at[j], w_recv.at[j], sibling) for j, (src, dst) in enumerate(weight_pairs)]

    loads[5].wait()
    loads[6].wait()
    text_rows = text.shape[0]
    text_keys[pl.ds(0, text_rows), :] = text[:, 0, :]
    text_values[pl.ds(0, text_rows), :] = text[:, 1, :]
    text_keys[pl.ds(text_rows, TEXT_PAD - text_rows), :] = jnp.zeros((TEXT_PAD - text_rows, 128), BF16)
    text_values[pl.ds(text_rows, TEXT_PAD - text_rows), :] = jnp.zeros((TEXT_PAD - text_rows, 128), BF16)
    gains = gain[...]
    gain_rows = jnp.concatenate([gains, gains], axis=1)
    lane = lax.broadcasted_iota(jnp.int32, (1, 128), 1)
    head_masks = ((lane < HD).astype(BF16), (lane >= HD).astype(BF16))

    def root_norm(values, gain_row):
        squares = values * values
        first = jnp.sum(jnp.where(lane < HD, squares, 0.0), axis=1, keepdims=True)
        second = jnp.sum(jnp.where(lane < HD, 0.0, squares), axis=1, keepdims=True)
        mean = jnp.where(lane < HD, first, second) * (1.0 / HD)
        return values * lax.rsqrt(mean + EPSILON) * gain_row

    for j in (2, 3, 4):
        loads[j].wait()
    for copy in shared[:3]:
        copy.wait()
    projected = project(g1, gather1, lambda left, cols: jnp.dot(left, wi[cols, :], preferred_element_type=F32))

    kvs[:, 0:128] = root_norm(projected[:, 512:640], gain_rows[1:2]).astype(BF16)
    kvs[:, 128:256] = projected[:, 640:768].astype(BF16)
    kvr[0, 0:half, 0:128] = root_norm(projected[:, 128:256], gain_rows[1:2]).astype(BF16)
    kvr[0, 0:half, 128:256] = projected[:, 256:384].astype(BF16)
    lower, upper = pl.ds(0, half), pl.ds(half, half)
    kv_copies = {}
    for dc in (1, 3, 2):
        back = 4 - dc
        kv_copies[back] = [
            send(kvr.at[0, lower], kvr.at[back, lower], kv_send.at[dc, 0], kv_recv.at[back, 0], device(dc=dc)),
            send(kvs, kvr.at[back, upper], kv_send.at[dc, 1], kv_recv.at[back, 1], device(dk=1, dc=dc)),
        ]
    own_pair = send(kvs, kvr.at[0, upper], kv_send.at[0, 1], kv_recv.at[0, 1], sibling)
    qs[...] = (root_norm(projected[:, 384:512], gain_rows[0:1]) * HD ** (-0.5)).astype(BF16)
    q_copy = send(qs, qb.at[upper], q_send, q_recv, sibling)
    qb[lower, :] = (root_norm(projected[:, 0:128], gain_rows[0:1]) * HD ** (-0.5)).astype(BF16)

    def attend(keys, values, chunks, keep=None):
        for n in chunks:
            rows = pl.ds(n * half, half)
            query = qb[pl.ds((n % 2) * half, half), :] * head_masks[n // 2]
            scores = nt_dot(query, keys)
            if keep is not None:
                scores = jnp.where(keep, scores, MASKED)
            old = s_max[rows, :]
            new = jnp.maximum(old, jnp.max(scores, axis=1, keepdims=True))
            factor = jnp.exp(old - new)
            weights = jnp.exp(scores - new[:, 0:1])
            s_max[rows, :] = new
            s_sum[rows, :] = s_sum[rows, :] * factor + jnp.sum(weights, axis=1, keepdims=True)
            s_acc[rows, :] = s_acc[rows, :] * factor + jnp.dot(
                weights.astype(BF16), values, preferred_element_type=F32
            )

    s_max[...] = jnp.full_like(s_max, MASKED)
    s_sum[...] = jnp.zeros_like(s_sum)
    s_acc[...] = jnp.zeros_like(s_acc)
    keep = lax.broadcasted_iota(jnp.int32, (1, TEXT_PAD), 1) < length_ref[0]
    attend(text_keys[...], text_values[...], (0, 2), keep)
    q_copy.wait()
    attend(text_keys[...], text_values[...], (1, 3), keep)
    own_pair.wait()
    attend(kvr[0, :, 0:128], kvr[0, :, 128:256], (1, 3, 0, 2))
    for dc in (1, 3):
        for copy in kv_copies[dc]:
            copy.wait()
        attend(kvr[dc, :, 0:128], kvr[dc, :, 128:256], (1, 3, 0, 2))
    for copy in kv_copies[2]:
        copy.wait()

    def attended(parity):
        low, high = pl.ds(parity * half, half), pl.ds((2 + parity) * half, half)
        first = s_acc[low, :] / s_sum[low, :]
        second = s_acc[high, :] / s_sum[high, :]
        return jnp.where(lane < HD, first, second).astype(BF16)

    attend(kvr[2, :, 0:128], kvr[2, :, 128:256], (1, 3))
    ats[...] = attended(1)
    a_copy = send(ats, ab.at[:, pl.ds(128, 128)], a_send, a_recv, sibling)
    attend(kvr[2, :, 0:128], kvr[2, :, 128:256], (0, 2))
    ab[:, 0:128] = attended(0)
    loads[7].wait()
    shared[3].wait()
    a_copy.wait()

    columns = [(n, min(512, width - n)) for n in range(0, width, 512)]

    def scatter(left, weight, part, arrive, send_sems, recv_sems):
        copies = []
        for c, (start, size) in enumerate(columns):
            cols = pl.ds(start, size)
            part[:, cols] = jnp.dot(left, weight[:, cols], preferred_element_type=F32).astype(BF16)
            for n, (dz, dx) in enumerate(PEERS):
                src = part.at[pl.ds(slot_of(dz, dx) * tile, tile), cols]
                dst = arrive.at[pl.ds(slot_of(dz, -dx) * tile, tile), cols]
                copies.append(send(src, dst, send_sems.at[c, n], recv_sems.at[c, n], device(dz, dx)))
        return copies

    def collect(copies, part, arrive):
        for copy in copies:
            copy.wait()
        total = part[pl.ds(0, tile), :].astype(F32)
        for n in range(1, 8):
            total = total + arrive[pl.ds(n * tile, tile), :].astype(F32)
        return total

    scatter1 = scatter(ab[...], wo, p1, r1, r1_send, r1_recv)
    attention = collect(scatter1, p1, r1)
    middle = tok[...].astype(F32) + mod[2:3, :] * attention
    g2[pl.ds(0, tile), :] = modulate(middle, mod[3:4, :], mod[4:5, :])
    gather2 = spread(g2, g2_send, g2_recv)
    loads[8].wait()
    loads[9].wait()
    shared[4].wait()
    shared[5].wait()
    up = project(g2, gather2, lambda left, cols: nt_dot(left, wu[:, cols]))
    hidden = jax.nn.gelu(up, approximate=True).astype(BF16)
    scatter2 = scatter(hidden, wd, p2, r2, r2_send, r2_recv)
    feed = collect(scatter2, p2, r2)
    leaving = middle + mod[5:6, :] * feed
    out_tok[...] = leaving.astype(BF16)
    final_input = modulate(leaving, mod[6:7, :], mod[7:8, :])
    loads[10].wait()
    vraw[...] = nt_dot(final_input, wf[...])
    pairs_of_tokens = tile // 2
    vx[...] = jnp.concatenate(
        [vraw[pl.ds(0, pairs_of_tokens, stride=2), :], vraw[pl.ds(1, pairs_of_tokens, stride=2), :]], axis=1
    )
    v_copy = send(vx, vr, v_send, v_recv, device(other_item=True))
    out_mine[...] = vx[...]
    v_copy.wait()
    out_theirs[...] = vr[...]


def guide_kernel(step_ref, tok, raw_mine, raw_theirs, lat, out_tok, out_vel, out_lat):
    mine, theirs = raw_mine[...], raw_theirs[...]
    is_guided = jnp.full(mine.shape, lax.axis_index("item") % 2, jnp.int32) == 0
    guided = jnp.where(is_guided, mine, theirs)
    unguided = jnp.where(is_guided, theirs, mine)
    velocity = unguided + GUIDANCE * (guided - unguided)
    position = jnp.full(mine.shape, step_ref[0], jnp.int32).astype(F32)
    step_size = noise_level(position + 1.0) - noise_level(position)
    out_vel[...] = velocity
    out_lat[...] = lat[...] + step_size * velocity
    out_tok[...] = tok[...]


def on_device(
    tokens,
    text_keys_values,
    text_length,
    modulation,
    input_weight,
    norm_gain,
    output_weight,
    up_weight,
    down_weight,
    final_weight,
    step_index,
    latent,
):
    tile = tokens.shape[1] * tokens.shape[2]
    width = tokens.shape[3]
    ff = up_weight.shape[1]
    half = 8 * tile
    chunks = -(-width // 512)
    operands = (
        text_length,
        tokens.reshape(tile, width),
        text_keys_values.reshape(text_keys_values.shape[1:]),
        modulation.reshape(8, width),
        input_weight.transpose(1, 0, 2),
        norm_gain,
        output_weight,
        up_weight.T,
        down_weight,
        final_weight.T,
    )
    latent_rows = latent.reshape(-1, 128)
    lat_shape = latent_rows.shape
    vmem = pltpu.VMEM
    dma = pltpu.SemaphoreType.DMA
    scratch = [
        vmem((tile, width), BF16),
        vmem(operands[2].shape, BF16),
        vmem((8, width), F32),
        vmem((width, 768), BF16),
        vmem(norm_gain.shape, F32),
        vmem((256, width), BF16),
        vmem((2 * ff, width), BF16),
        vmem((2 * ff, width), BF16),
        vmem((final_weight.shape[1], width), BF16),
    ]
    scratch += [vmem((half, width), BF16)] * 6
    scratch += [
        vmem((4, 2 * half, 256), BF16),
        vmem((half, 256), BF16),
        vmem((2 * half, 128), BF16),
        vmem((half, 128), BF16),
        vmem((half, 256), BF16),
        vmem((half, 128), BF16),
        vmem((4 * half, 128), F32),
        vmem((4 * half, 128), F32),
        vmem((4 * half, 128), F32),
        vmem((tile, final_weight.shape[1]), F32),
        vmem(lat_shape, F32),
        vmem(lat_shape, F32),
        vmem((TEXT_PAD, 128), BF16),
        vmem((TEXT_PAD, 128), BF16),
    ]
    scratch += [dma((12,)), dma((6,)), dma((6,)), dma((4, 7)), dma((4, 7)), dma((4, 2)), dma((4, 2))]
    scratch += [dma, dma, dma, dma, dma((chunks, 7)), dma((chunks, 7)), dma((4, 7)), dma((4, 7))]
    scratch += [dma((chunks, 7)), dma((chunks, 7)), dma, dma]
    smem = pl.BlockSpec(memory_space=pltpu.SMEM)
    hbm = pl.BlockSpec(memory_space=pl.ANY)
    whole = pl.BlockSpec(memory_space=pltpu.VMEM)
    outs = (
        jax.ShapeDtypeStruct((tile, width), BF16),
        jax.ShapeDtypeStruct(lat_shape, F32),
        jax.ShapeDtypeStruct(lat_shape, F32),
    )
    leaving, mine, theirs = pl.pallas_call(
        layer_kernel,
        out_shape=outs,
        in_specs=[smem] + [hbm] * 9,
        out_specs=(whole, whole, whole),
        scratch_shapes=scratch,
        compiler_params=pltpu.CompilerParams(
            collective_id=0, has_side_effects=True, vmem_limit_bytes=56 * 1024 * 1024
        ),
        name="layer",
    )(*operands)
    tokens_out, velocity, latent_next = pl.pallas_call(
        guide_kernel,
        out_shape=outs,
        in_specs=[smem, whole, whole, whole, whole],
        out_specs=(whole, whole, whole),
        name="guide",
    )(step_index, leaving, mine, theirs, latent_rows)
    return (tokens_out.reshape(tokens.shape), velocity.reshape(latent.shape), latent_next.reshape(latent.shape))


def solution(mesh):
    in_specs = (
        P("item", "row", "col", None),
        P("item", None, None, "row"),
        P("item"),
        P("item", None, None),
        P(None, None, "row"),
        P(),
        P("row", None),
        P(None, "row"),
        P("row", None),
        P(),
        P(),
        P("item", "row", "col"),
    )
    out_specs = (P("item", "row", "col", None), P("item", "row", "col"), P("item", "row", "col"))
    return jax.shard_map(
        on_device, mesh=mesh, in_specs=in_specs, out_specs=out_specs, check_vma=False
    )
```

```python
import functools

import jax
import jax.numpy as jnp
from jax import lax
from jax.experimental import pallas as pl
from jax.experimental.pallas import tpu as pltpu
from jax.sharding import PartitionSpec as P

HD = 64
STEPS = 28
EPSILON = 1e-06
SHIFT_FACTOR = 3.0
GUIDANCE = 4.5
MASKED = -1e30
MESH = pl.DeviceIdType.MESH
BF16 = jnp.bfloat16
F32 = jnp.float32

PEERS = ((1, 2), (0, 2), (1, 1), (1, 3), (0, 1), (0, 3), (1, 0))
AG1, RS1, AG2, RS2 = "relay", "relay", "direct", "direct"
AG2_COLS = (640, 640, 640, 512)
RS2_COLS = (896, 768, 768)
TEXT_PAD = 160


def slot_of(dz, dx):
    return (dz % 2) * 4 + dx % 4


def layer_norm(values):
    center = values - jnp.mean(values, axis=-1, keepdims=True)
    spread = jnp.mean(center * center, axis=-1, keepdims=True)
    return center * lax.rsqrt(spread + EPSILON)


def modulate(values, shift_term, scale_term):
    return (layer_norm(values) * (1.0 + scale_term) + shift_term).astype(BF16)


def noise_level(position):
    linear = 1.0 - position / STEPS
    return SHIFT_FACTOR * linear / (1.0 + (SHIFT_FACTOR - 1.0) * linear)


def nt_dot(left, right):
    return lax.dot_general(left, right, (((1,), (1,)), ((), ())), preferred_element_type=F32)


def layer_kernel(
    length_hbm, step_hbm, tok_hbm, text_hbm, mod_hbm, win_hbm, gain_hbm, wo_hbm, wu_hbm, wd_hbm, wf_hbm, lat_hbm,
    out_tok, out_vel, out_lat,
    length_ref, step_ref, lat, tok, text, mod, wi, gain, wo, wu, wut, wd, wf,
    g1, g2, p1, p2, r1, r2, kvr, kvs, qb, qs, ab, ats, s_max, s_sum, s_acc, vraw, vx, vr, text_keys, text_values, mid,
    local_sem, w_send, w_recv, g1_send, g1_recv, kv_send, kv_recv, q_send, q_recv, a_send, a_recv,
    r1_send, r1_recv, g2_send, g2_recv, r2_send, r2_recv, v_send, v_recv,
):
    tile, width = tok.shape
    part = tile // 2
    rows = 8 * part
    half = tile * 8
    ff = wu_hbm.shape[0]
    row = lax.axis_index("row")
    col = lax.axis_index("col")
    item = lax.axis_index("item")
    z, x, k = row // 8, (row // 2) % 4, row % 2

    def device(dz=0, dx=0, dk=0, dc=0, other_item=False):
        row_to = ((z + dz) % 2) * 8 + ((x + dx) % 4) * 2 + (k + dk) % 2
        item_to = item + 1 - 2 * (item % 2) if other_item else item
        return (row_to, (col + dc) % 4, item_to)

    def send(src, dst, send_sem, recv_sem, to):
        copy = pltpu.make_async_remote_copy(
            src_ref=src, dst_ref=dst, send_sem=send_sem, recv_sem=recv_sem, device_id=to, device_id_type=MESH
        )
        copy.start()
        return copy

    pairs = [(tok_hbm, tok), (mod_hbm, mod)]
    pairs += [(win_hbm.at[j], wi.at[:, pl.ds(128 * j, 128)]) for j in range(3)]
    pairs += [(text_hbm, text), (gain_hbm, gain), (wo_hbm, wo.at[pl.ds(0, 128)])]
    pairs += [(wu_hbm, wu), (wd_hbm, wd.at[pl.ds(0, ff)]), (wf_hbm, wf), (lat_hbm, lat)]
    pairs += [(length_hbm, length_ref), (step_hbm, step_ref)]
    loads = [pltpu.make_async_copy(src, dst, local_sem.at[j]) for j, (src, dst) in enumerate(pairs)]
    for load in loads:
        load.start()

    friends = [device(dz, dx) for dz, dx in PEERS] + [device(dk=1), device(other_item=True)]
    friends += [device(dk=dk, dc=dc) for dc in (1, 2, 3) for dk in (0, 1)]
    barrier = pltpu.get_barrier_semaphore()
    for friend in friends:
        pl.semaphore_signal(barrier, inc=1, device_id=friend, device_id_type=MESH)

    loads[0].wait()
    loads[1].wait()
    states = tok[...].astype(F32)
    attn_input = modulate(states, mod[0:1, :], mod[1:2, :])
    for h in range(2):
        g1[h, 0:part, :] = attn_input[part * h : part * (h + 1)]
    pl.semaphore_wait(barrier, len(friends))

    def columns_of(sizes):
        starts = [sum(sizes[:n]) for n in range(len(sizes))]
        return [pl.ds(start, size) for start, size in zip(starts, sizes)]

    every = slice(None)

    def block(slot, region):
        return (region[0], pl.ds(slot * part, part), region[1])

    def hop(buf, slot, to_buf, to_slot, region, sems, n, dz, dx):
        return send(
            buf.at[block(slot, region)], to_buf.at[block(to_slot, region)], sems[0].at[n], sems[1].at[n], device(dz, dx)
        )

    def spread(buf, region, sems):
        steps = ((0, 2), (1, 0), (0, 1), (0, 3))
        return [hop(buf, 0, buf, slot_of(dz, -dx), region, sems, n, dz, dx) for n, (dz, dx) in enumerate(steps)]

    def pass_on(buf, region, sems, started):
        across, over_z, left, right = started
        over_z.wait_recv()
        z_slot = slot_of(1, 0)
        more = [
            hop(buf, z_slot, buf, slot_of(1, 3), region, sems, 4, 0, 1),
            hop(buf, z_slot, buf, slot_of(1, 1), region, sems, 5, 0, 3),
        ]
        across.wait_recv()
        more.append(hop(buf, slot_of(0, 2), buf, slot_of(1, 2), region, sems, 6, 1, 0))

        def finish():
            over_z.wait_send()
            across.wait_send()
            for copy in [left, right] + more:
                copy.wait()

        return finish

    def scatter(buf, inbox, region, sems):
        return [
            hop(buf, slot_of(1, 1), inbox, 0, region, sems, 0, 0, 1),
            hop(buf, slot_of(1, 3), inbox, 1, region, sems, 1, 0, 3),
            hop(buf, slot_of(1, 2), inbox, 2, region, sems, 2, 1, 0),
            hop(buf, slot_of(0, 1), inbox, 3, region, sems, 3, 0, 1),
            hop(buf, slot_of(0, 3), inbox, 4, region, sems, 4, 0, 3),
        ]

    def sum_on(buf, inbox, region, sems, started):
        started[0].wait_recv()
        started[1].wait_recv()
        z_block, far_block = block(slot_of(1, 0), region), block(slot_of(0, 2), region)
        buf[z_block] = (
            buf[z_block].astype(F32) + inbox[block(0, region)].astype(F32) + inbox[block(1, region)].astype(F32)
        ).astype(BF16)
        more = [hop(buf, slot_of(1, 0), inbox, 5, region, sems, 5, 1, 0)]
        started[2].wait_recv()
        buf[far_block] = (buf[far_block].astype(F32) + inbox[block(2, region)].astype(F32)).astype(BF16)
        more.append(hop(buf, slot_of(0, 2), inbox, 6, region, sems, 6, 0, 2))

        def finish():
            for copy in started[:3]:
                copy.wait_send()
            for copy in started[3:] + more:
                copy.wait()

        return finish

    def spread_direct(buf, region, sems):
        return [hop(buf, 0, buf, slot_of(dz, -dx), region, sems, n, dz, dx) for n, (dz, dx) in enumerate(PEERS)]

    def scatter_direct(buf, inbox, region, sems):
        return [
            hop(buf, slot_of(dz, dx), inbox, slot_of(dz, -dx), region, sems, n, dz, dx)
            for n, (dz, dx) in enumerate(PEERS)
        ]

    def finish_direct(started):
        def finish():
            for copy in started:
                copy.wait()

        return finish

    def gather_start(how, buf, region, sems):
        return (spread if how == "relay" else spread_direct)(buf, region, sems)

    def gather_go(how, buf, region, sems, started):
        return pass_on(buf, region, sems, started) if how == "relay" else finish_direct(started)

    def scatter_start(how, buf, inbox, region, sems):
        return (scatter if how == "relay" else scatter_direct)(buf, inbox, region, sems)

    def scatter_go(how, buf, inbox, region, sems, started):
        return sum_on(buf, inbox, region, sems, started) if how == "relay" else finish_direct(started)

    def total_of(how, buf, inbox, region):
        total = buf[block(0, region)].astype(F32)
        for n in range(3, 7) if how == "relay" else range(1, 8):
            total = total + inbox[block(n, region)].astype(F32)
        return total

    halves = [(0, every), (1, every)]
    gather1_sems = [(g1_send.at[h], g1_recv.at[h]) for h in range(2)]
    gather1 = [gather_start(AG1, g1, halves[h], gather1_sems[h]) for h in range(2)]
    sibling = device(dk=1)
    weight_pairs = [(win_hbm.at[j], wi.at[:, pl.ds(384 + 128 * j, 128)]) for j in range(3)]
    weight_pairs += [(wo_hbm, wo.at[pl.ds(128, 128)]), (wd_hbm, wd.at[pl.ds(ff, ff)])]
    shared = [send(src, dst, w_send.at[j], w_recv.at[j], sibling) for j, (src, dst) in enumerate(weight_pairs)]

    loads[5].wait()
    loads[6].wait()
    text_rows = text.shape[0]
    text_keys[pl.ds(0, text_rows), :] = text[:, 0, :]
    text_values[pl.ds(0, text_rows), :] = text[:, 1, :]
    text_keys[pl.ds(text_rows, TEXT_PAD - text_rows), :] = jnp.zeros((TEXT_PAD - text_rows, 128), BF16)
    text_values[pl.ds(text_rows, TEXT_PAD - text_rows), :] = jnp.zeros((TEXT_PAD - text_rows, 128), BF16)
    gains = gain[...]
    gain_rows = jnp.concatenate([gains, gains], axis=1)
    lane = lax.broadcasted_iota(jnp.int32, (1, 128), 1)
    head_masks = ((lane < HD).astype(BF16), (lane >= HD).astype(BF16))

    def root_norm(values, gain_row):
        squares = values * values
        first = jnp.sum(jnp.where(lane < HD, squares, 0.0), axis=1, keepdims=True)
        second = jnp.sum(jnp.where(lane < HD, 0.0, squares), axis=1, keepdims=True)
        mean = jnp.where(lane < HD, first, second) * (1.0 / HD)
        return values * lax.rsqrt(mean + EPSILON) * gain_row

    gather1 = [gather_go(AG1, g1, halves[h], gather1_sems[h], gather1[h]) for h in range(2)]
    loads[8].wait()
    for n in range(0, width, 128):
        wut[0, pl.ds(n, 128), :] = wu[:, pl.ds(n, 128)].T
    shared.append(send(wut.at[0], wut.at[1], w_send.at[5], w_recv.at[5], sibling))
    for j in (2, 3, 4):
        loads[j].wait()
    for copy in shared[:3]:
        copy.wait()
    places = (0, 1, 3, 2)
    kv_copies = [{}, {}]
    own_pairs = []
    q_copies = []
    for h in range(2):
        gather1[h]()
        projected = jnp.dot(g1[h], wi[...], preferred_element_type=F32)
        mine, other = pl.ds(0, rows), pl.ds(rows, rows)
        kvs[h, :, 0:128] = root_norm(projected[:, 512:640], gain_rows[1:2]).astype(BF16)
        kvs[h, :, 128:256] = projected[:, 640:768].astype(BF16)
        kvr[h, 0, mine, 0:128] = root_norm(projected[:, 128:256], gain_rows[1:2]).astype(BF16)
        kvr[h, 0, mine, 128:256] = projected[:, 256:384].astype(BF16)
        for dc in (1, 3, 2):
            back = 4 - dc
            kv_copies[h][back] = [
                send(
                    kvr.at[h, 0, mine], kvr.at[h, places[back], mine], kv_send.at[h, dc, 0],
                    kv_recv.at[h, back, 0], device(dc=dc),
                ),
                send(
                    kvs.at[h], kvr.at[h, places[back], other], kv_send.at[h, dc, 1],
                    kv_recv.at[h, back, 1], device(dk=1, dc=dc),
                ),
            ]
        own_pairs.append(send(kvs.at[h], kvr.at[h, 0, other], kv_send.at[h, 0, 1], kv_recv.at[h, 0, 1], sibling))
        here = pl.ds(h * rows, rows)
        qs[here, :] = (root_norm(projected[:, 384:512], gain_rows[0:1]) * HD ** (-0.5)).astype(BF16)
        q_copies.append(
            send(qs.at[here], qb.at[pl.ds(half + h * rows, rows)], q_send.at[h], q_recv.at[h], sibling)
        )
        qb[here, :] = (root_norm(projected[:, 0:128], gain_rows[0:1]) * HD ** (-0.5)).astype(BF16)

    def attend(keys, values, blocks, keep=None):
        at = [pl.ds(n * half, half) for n in blocks]
        scores = [nt_dot(qb[pl.ds((n % 2) * half, half), :] * head_masks[n // 2], keys) for n in blocks]
        if keep is not None:
            scores = [jnp.where(keep, score, MASKED) for score in scores]
        old = [s_max[w, :] for w in at]
        old_sum = [s_sum[w, :] for w in at]
        old_acc = [s_acc[w, :] for w in at]
        new = [jnp.maximum(o, jnp.max(score, axis=1, keepdims=True)) for o, score in zip(old, scores)]
        factor = [jnp.exp(o - n) for o, n in zip(old, new)]
        weights = [jnp.exp(score - n[:, 0:1]) for score, n in zip(scores, new)]
        new_sum = [o * f + jnp.sum(w, axis=1, keepdims=True) for o, f, w in zip(old_sum, factor, weights)]
        new_acc = [
            o * f + jnp.dot(w.astype(BF16), values, preferred_element_type=F32)
            for o, f, w in zip(old_acc, factor, weights)
        ]
        for n, w in enumerate(at):
            s_max[w, :] = new[n]
            s_sum[w, :] = new_sum[n]
            s_acc[w, :] = new_acc[n]

    def attend_places(h, first, count, blocks):
        for_keys = kvr[h, first : first + count, :, 0:128].reshape(count * half, 128)
        for_values = kvr[h, first : first + count, :, 128:256].reshape(count * half, 128)
        attend(for_keys, for_values, blocks)

    s_max[...] = jnp.full_like(s_max, MASKED)
    s_sum[...] = jnp.zeros_like(s_sum)
    s_acc[...] = jnp.zeros_like(s_acc)
    loads[12].wait()
    keep = lax.broadcasted_iota(jnp.int32, (1, TEXT_PAD), 1) < length_ref[0]
    everyone = (1, 3, 0, 2)
    for copy in q_copies:
        copy.wait()
    attend(text_keys[...], text_values[...], everyone, keep)
    for copy in [own_pairs[0]] + kv_copies[0][1] + kv_copies[0][3] + kv_copies[0][2]:
        copy.wait()
    attend_places(0, 0, 4, everyone)
    for copy in [own_pairs[1]] + kv_copies[1][1] + kv_copies[1][3]:
        copy.wait()
    attend_places(1, 0, 3, everyone)
    for copy in kv_copies[1][2]:
        copy.wait()

    def attended(parity):
        low, high = pl.ds(parity * half, half), pl.ds((2 + parity) * half, half)
        first = s_acc[low, :] / s_sum[low, :]
        second = s_acc[high, :] / s_sum[high, :]
        return jnp.where(lane < HD, first, second).astype(BF16)

    attend_places(1, 3, 1, (1, 3))
    ats[...] = attended(1)
    a_copy = send(ats, ab.at[:, pl.ds(128, 128)], a_send, a_recv, sibling)
    attend_places(1, 3, 1, (0, 2))
    ab[:, 0:128] = attended(0)
    loads[7].wait()
    shared[3].wait()

    columns = [pl.ds(n, min(512, width - n)) for n in range(0, width, 512)]

    own = ab[:, 0:128]
    own_terms = [jnp.dot(own, wo[0:128, cols], preferred_element_type=F32) for cols in columns]
    a_copy.wait()
    other_heads = ab[:, 128:256]
    for cols, own_term in zip(columns, own_terms):
        term = (own_term + jnp.dot(other_heads, wo[128:256, cols], preferred_element_type=F32)).astype(BF16)
        p1[0, :, cols] = term[0:rows]
        p1[1, :, cols] = term[rows:half]
    scatter1_sems = [(r1_send.at[h], r1_recv.at[h]) for h in range(2)]
    scatter1 = [scatter_start(RS1, p1, r1, halves[h], scatter1_sems[h]) for h in range(2)]
    scatter1 = [scatter_go(RS1, p1, r1, halves[h], scatter1_sems[h], scatter1[h]) for h in range(2)]
    regions = [(0, every)] + [(1, cols) for cols in columns_of(AG2_COLS)]
    gather2_sems = [(g2_send.at[n], g2_recv.at[n]) for n in range(len(regions))]
    gather2 = []
    for h in range(2):
        scatter1[h]()
        attention = total_of(RS1, p1, r1, halves[h])
        middle = tok[pl.ds(part * h, part), :].astype(F32) + mod[2:3, :] * attention
        mid[pl.ds(part * h, part), :] = middle
        g2[h, 0:part, :] = modulate(middle, mod[3:4, :], mod[4:5, :])
        for n in range(1) if h == 0 else range(1, len(regions)):
            gather2.append(gather_start(AG2, g2, regions[n], gather2_sems[n]))
    gather2 = [gather_go(AG2, g2, regions[n], gather2_sems[n], gather2[n]) for n in range(len(regions))]
    loads[9].wait()
    shared[4].wait()
    shared[5].wait()
    gather2[0]()
    up = [jnp.zeros((half, ff), F32)] * 2
    for n, (_, cols) in list(enumerate(regions))[1:]:
        gather2[n]()
        feed_input = g2[:, :, cols].reshape(half, cols.size)
        up = [up[j] + jnp.dot(feed_input, wut[j, cols, :], preferred_element_type=F32) for j in range(2)]
    hidden = [jax.nn.gelu(u, approximate=True).astype(BF16) for u in up]
    scatter2 = []
    wide = [(every, cols) for cols in columns_of(RS2_COLS)]
    scatter2_sems = [(r2_send.at[c], r2_recv.at[c]) for c in range(len(wide))]
    for c in range(len(wide)):
        cols = wide[c][1]
        term = jnp.dot(hidden[0], wd[pl.ds(0, ff), cols], preferred_element_type=F32)
        term = (term + jnp.dot(hidden[1], wd[pl.ds(ff, ff), cols], preferred_element_type=F32)).astype(BF16)
        p2[0, :, cols] = term[0:rows]
        p2[1, :, cols] = term[rows:half]
        scatter2.append(scatter_start(RS2, p2, r2, wide[c], scatter2_sems[c]))
    scatter2 = [scatter_go(RS2, p2, r2, wide[c], scatter2_sems[c], scatter2[c]) for c in range(len(wide))]
    for finish in scatter2:
        finish()
    feed = total_of(RS2, p2, r2, (every, every)).reshape(tile, width)
    middle = mid[...]
    leaving = middle + mod[5:6, :] * feed
    out_tok[...] = leaving.astype(BF16)
    final_input = modulate(leaving, mod[6:7, :], mod[7:8, :])
    loads[10].wait()
    vraw[...] = nt_dot(final_input, wf[...])
    pairs_of_tokens = tile // 2
    vx[...] = jnp.concatenate(
        [vraw[pl.ds(0, pairs_of_tokens, stride=2), :], vraw[pl.ds(1, pairs_of_tokens, stride=2), :]], axis=1
    )
    v_copy = send(vx, vr, v_send, v_recv, device(other_item=True))
    loads[11].wait()
    loads[13].wait()
    mine = vx[...]
    is_guided = jnp.full(mine.shape, item % 2, jnp.int32) == 0
    position = jnp.full(mine.shape, step_ref[0], jnp.int32).astype(F32)
    step_size = noise_level(position + 1.0) - noise_level(position)
    v_copy.wait()
    theirs = vr[...]
    guided = jnp.where(is_guided, mine, theirs)
    unguided = jnp.where(is_guided, theirs, mine)
    velocity = unguided + GUIDANCE * (guided - unguided)
    out_vel[...] = velocity
    out_lat[...] = lat[...] + step_size * velocity


def copy_kernel(tok, vel, lat, out_tok, out_vel, out_lat):
    out_tok[...] = tok[...]
    out_vel[...] = vel[...]
    out_lat[...] = lat[...]


def on_device(
    tokens,
    text_keys_values,
    text_length,
    modulation,
    input_weight,
    norm_gain,
    output_weight,
    up_weight,
    down_weight,
    final_weight,
    step_index,
    latent,
):
    tile = tokens.shape[1] * tokens.shape[2]
    width = tokens.shape[3]
    ff = up_weight.shape[1]
    half = 8 * tile
    operands = (
        text_length,
        step_index,
        tokens.reshape(tile, width),
        text_keys_values.reshape(text_keys_values.shape[1:]),
        modulation.reshape(8, width),
        input_weight.transpose(1, 0, 2),
        norm_gain,
        output_weight,
        up_weight.T,
        down_weight,
        final_weight.T,
        latent.reshape(-1, 128),
    )
    lat_shape = operands[-1].shape
    vmem = pltpu.VMEM
    dma = pltpu.SemaphoreType.DMA
    smem = pltpu.SMEM
    scratch = [
        smem((1,), jnp.int32),
        smem((1,), jnp.int32),
        vmem(lat_shape, F32),
        vmem((tile, width), BF16),
        vmem(operands[3].shape, BF16),
        vmem((8, width), F32),
        vmem((width, 768), BF16),
        vmem(norm_gain.shape, F32),
        vmem((256, width), BF16),
        vmem((ff, width), BF16),
        vmem((2, width, ff), BF16),
        vmem((2 * ff, width), BF16),
        vmem((final_weight.shape[1], width), BF16),
    ]
    scratch += [vmem((2, half // 2, width), BF16)] * 6
    scratch += [
        vmem((2, 4, half, 256), BF16),
        vmem((2, half // 2, 256), BF16),
        vmem((2 * half, 128), BF16),
        vmem((half, 128), BF16),
        vmem((half, 256), BF16),
        vmem((half, 128), BF16),
        vmem((4 * half, 128), F32),
        vmem((4 * half, 128), F32),
        vmem((4 * half, 128), F32),
        vmem((tile, final_weight.shape[1]), F32),
        vmem(lat_shape, F32),
        vmem(lat_shape, F32),
        vmem((TEXT_PAD, 128), BF16),
        vmem((TEXT_PAD, 128), BF16),
        vmem((tile, width), F32),
    ]
    scratch += [dma((14,)), dma((6,)), dma((6,)), dma((2, 7)), dma((2, 7)), dma((2, 4, 2)), dma((2, 4, 2))]
    scratch += [dma((2,)), dma((2,)), dma, dma, dma((2, 7)), dma((2, 7)), dma((1 + len(AG2_COLS), 7)), dma((1 + len(AG2_COLS), 7))]
    scratch += [dma((len(RS2_COLS), 7)), dma((len(RS2_COLS), 7)), dma, dma]
    hbm = pl.BlockSpec(memory_space=pltpu.HBM)
    whole = pl.BlockSpec(memory_space=pltpu.VMEM)
    outs = (
        jax.ShapeDtypeStruct((tile, width), BF16),
        jax.ShapeDtypeStruct(lat_shape, F32),
        jax.ShapeDtypeStruct(lat_shape, F32),
    )
    results = pl.pallas_call(
        layer_kernel,
        out_shape=outs,
        in_specs=[hbm] * 12,
        out_specs=(whole, whole, whole),
        scratch_shapes=scratch,
        compiler_params=pltpu.CompilerParams(
            collective_id=0, has_side_effects=True, vmem_limit_bytes=56 * 1024 * 1024
        ),
        name="layer",
    )(*operands)
    tokens_out, velocity, latent_next = pl.pallas_call(
        copy_kernel,
        out_shape=outs,
        in_specs=[whole] * 3,
        out_specs=(whole, whole, whole),
        name="copy",
    )(*results)
    return (tokens_out.reshape(tokens.shape), velocity.reshape(latent.shape), latent_next.reshape(latent.shape))


def solution(mesh):
    in_specs = (
        P("item", "row", "col", None),
        P("item", None, None, "row"),
        P("item"),
        P("item", None, None),
        P(None, None, "row"),
        P(),
        P("row", None),
        P(None, "row"),
        P("row", None),
        P(),
        P(),
        P("item", "row", "col"),
    )
    out_specs = (P("item", "row", "col", None), P("item", "row", "col"), P("item", "row", "col"))
    return jax.shard_map(
        on_device, mesh=mesh, in_specs=in_specs, out_specs=out_specs, check_vma=False
    )
```
